32 devices in a mesh: ladder: 4 (over x, core), space: 8 (over z, y).
Axes of the slice: x: 2, y: 2, z: 4, core: 2. Of those that a mesh axis runs over, the one named last changes fastest.
Arguments:
- initial: float32 [4, 256, 2048], P('ladder', 'space'), may hold values from -1.2 to 1.2
- mobility: float32 [256, 2048], P('space'), may hold values from 0.1 to 0.5
- tilt: float32 [256, 2048], P('space'), may hold values from -0.5 to 0.5
- drift: float32 [2048], replicated, may hold values from -0.6 to 0.6
- mix_weights: float32 [4, 2], P('ladder'), may hold values from 0.2 to 0.4
Outputs:
- path: float32 [4, 256, 2048], P('ladder', 'space')
The draws below stay inside these ranges and needn't reach their ends.
All inputs are finite; a program needn't handle non-finite values.
Results may differ from the reference program's by a relative error of at most 0.00002.
Values sent between devices are 32-bit elements; how exact they have to be, the bound alone decides.
A program may use at most 64 MiB of HBM per device.

```python
import math
import jax
import jax.numpy as jnp

COLS = 2048
STEPS = 12
CYCLES = 2
IMAGES = 4
ROWS = 256


def steps_of(rng, extent, cuts, smallest, largest):
    def one(axis_at, parts):
        heights = jax.random.uniform(jax.random.fold_in(jax.random.fold_in(rng, 6), axis_at), (parts,), jnp.float32, smallest / len(cuts), largest / len(cuts))
        return jnp.repeat(jnp.exp(heights), extent[axis_at] // parts).reshape((-1,) + (1,) * (len(extent) - axis_at - 1))

    loudness = one(*cuts[0])
    for cut in cuts[1:]:
        loudness = loudness * one(*cut)
    return loudness


def setup_inputs(seed: int = 0) -> dict:
    splits = jax.random.split(jax.random.key(seed), 6)
    initial = jnp.clip(jax.random.uniform(splits[0], (IMAGES, ROWS, COLS), jnp.float32, -1.2, 1.2) * steps_of(splits[0], (IMAGES, ROWS, COLS), ((0, 4), (1, 8)), -0.4, 0.0), -1.2, 1.2)
    mobility = jnp.clip(jnp.exp(math.log(0.5) - 1.609438 * jax.random.uniform(splits[1], (ROWS, COLS), jnp.float32) ** steps_of(splits[1], (ROWS, COLS), ((0, 8),), -0.2, 0.2)), 0.1, 0.5)
    tilt = jnp.clip(jax.random.uniform(splits[2], (ROWS, COLS), jnp.float32, -0.5, 0.5) * steps_of(splits[2], (ROWS, COLS), ((0, 8),), -0.4, 0.0), -0.5, 0.5)
    drift = jnp.clip(jax.random.uniform(splits[3], (COLS,), jnp.float32, -0.6, 0.6), -0.6, 0.6)
    mix_weights = jnp.clip(0.2 + 0.2 * jax.random.uniform(splits[4], (IMAGES, 2), jnp.float32) ** steps_of(splits[4], (IMAGES, 2), ((0, 4),), -0.2, 0.2), 0.2, 0.4)
    return dict(initial=initial, mobility=mobility, tilt=tilt, drift=drift, mix_weights=mix_weights)


def advance(field, mobility, tilt, rising, falling):
    below = jnp.roll(field, 1, -2)
    above = jnp.roll(field, -1, -2)
    vertical = below + above
    horizontal = jnp.roll(field, 1, -1) + jnp.roll(field, -1, -1)
    laplace = vertical + horizontal - 4.0 * field
    transport = rising * (field - below) + falling * (above - field)
    return field + 0.1 * mobility * (laplace + field - field * field * field + tilt) - transport


def reference(initial, mobility, tilt, drift, mix_weights):
    field = initial
    rising = jnp.maximum(drift, 0.0)[None, None, :]
    falling = jnp.minimum(drift, 0.0)[None, None, :]
    lower_w = mix_weights[:, 0][:, None, None]
    upper_w = mix_weights[:, 1][:, None, None]
    for cycle in range(CYCLES):
        for step in range(STEPS):
            field = advance(field, mobility[None], tilt[None], rising, falling)
        lower = jnp.concatenate([field[:1], field[:-1]], axis=0)
        upper = jnp.concatenate([field[1:], field[-1:]], axis=0)
        field = (1.0 - lower_w - upper_w) * field + lower_w * lower + upper_w * upper
    return field
```

```python
import functools

import jax
import jax.numpy as jnp
from jax import lax
from jax.experimental import pallas as pl
from jax.experimental.pallas import tpu as pltpu
from jax.sharding import PartitionSpec as P

CYCLES = 2
DEPTH = 12
LANES = 128
SUBS = 8
CHUNK = 4
MESH = pl.DeviceIdType.MESH


def kernel(sizes, init_hbm, mob_hbm, tilt_hbm, drift_ref, mix_ref, out_hbm,
           stage, coef, fields, beside, ostage, load_sem, send_sem, recv_sem):
    n_ladder, n_space, height, halves, blocks = sizes
    place = lax.axis_index("ladder")
    slab = lax.axis_index("space")
    prev = lax.rem(slab + n_space - 1, n_space)
    following = lax.rem(slab + 1, n_space)
    core = lax.rem(place, 2)
    partner = place + 1 - 2 * core
    has_lower = place > 0
    has_upper = place < n_ladder - 1
    top, bottom = DEPTH, DEPTH + height
    full = height + 2 * DEPTH

    sources = (mob_hbm, tilt_hbm, init_hbm.at[0])
    loads = []
    for a, src in enumerate(sources):
        for j in range(blocks):
            copy = pltpu.make_async_copy(
                src.at[:, pl.ds(j * LANES, LANES)],
                stage.at[a, pl.ds(j * height, height), :],
                load_sem.at[a, j],
            )
            copy.start()
            loads.append(copy)

    barrier = pltpu.get_barrier_semaphore()
    for target in (prev, following):
        pl.semaphore_signal(barrier, inc=1, device_id={"space": target}, device_id_type=MESH)

    for target in (lax.rem(place + n_ladder - 1, n_ladder), lax.rem(place + 1, n_ladder)):
        pl.semaphore_signal(barrier, inc=1, device_id={"ladder": target}, device_id_type=MESH)

    def remote(index, src, dst, device):
        return pltpu.make_async_remote_copy(
            src_ref=src, dst_ref=dst, send_sem=send_sem.at[index], recv_sem=recv_sem.at[index],
            device_id=device, device_id_type=MESH)

    def spread(a, dst, scale):
        for r in range(height):
            for v in range(halves):
                tile = stage[a, pl.ds(v * height + r, SUBS, stride=halves * height), :]
                dst[top + r, v] = tile * scale if scale is not None else tile

    wide = DEPTH - 1
    for copy in loads[: 2 * blocks]:
        copy.wait()
    spread(0, coef.at[0], 0.1)
    spread(1, coef.at[1], None)

    pl.semaphore_wait(barrier, 4)

    coef_up = remote(0, coef.at[core, pl.ds(top, wide)], coef.at[core, pl.ds(bottom, wide)], {"space": prev})
    coef_down = remote(1, coef.at[core, pl.ds(bottom - wide, wide)], coef.at[core, pl.ds(1, wide)], {"space": following})
    coef_up.start()
    coef_down.start()
    for copy in loads[2 * blocks:]:
        copy.wait()
    spread(2, fields.at[0], None)

    def halo(index, f):
        up = remote(index, f.at[pl.ds(top, DEPTH)], f.at[pl.ds(bottom, DEPTH)], {"space": prev})
        down = remote(index + 1, f.at[pl.ds(bottom - DEPTH, DEPTH)], f.at[pl.ds(0, DEPTH)], {"space": following})
        return up, down

    halo_up, halo_down = halo(2, fields.at[0])
    halo_up.start()
    halo_down.start()

    lane = lax.broadcasted_iota(jnp.int32, (SUBS, LANES), 1)
    at_first = lane == 0
    at_last = lane == LANES - 1
    drifts = [drift_ref[pl.ds(v, SUBS, stride=halves), :] for v in range(halves)]
    speeds = [jnp.abs(u) for u in drifts]
    rises = [u > 0.0 for u in drifts]

    def rows(src, dst, lo, count):
        for first in range(0, count, CHUNK):
            many = min(CHUNK, count - first)
            base = lo + first
            tiles = [[src[base - 1 + r, v] for v in range(halves)] for r in range(many + 2)]
            for r in range(many):
                below, here, above = tiles[r], tiles[r + 1], tiles[r + 2]
                right = [pltpu.roll(here[v], 1, 1) for v in range(halves)]
                left = [pltpu.roll(here[v], LANES - 1, 1) for v in range(halves)]
                before = [pltpu.roll(right[-1], 1, 0)] + right[:-1]
                after = left[1:] + [pltpu.roll(left[0], SUBS - 1, 0)]
                for v in range(halves):
                    p = here[v]
                    side = jnp.where(at_first, before[v], right[v]) + jnp.where(at_last, after[v], left[v])
                    around = side + (below[v] + above[v]) + coef[1, base + r, v]
                    drive = around - p * (p * p + 3.0)
                    carried = jnp.where(rises[v], below[v], above[v]) - p
                    dst[base + r, v] = p + speeds[v] * carried + coef[0, base + r, v] * drive

    def level(cycle, k):
        return fields.at[3 * cycle + (0 if k == 0 else 1 + (k + 1) % 2)]

    def pyramid(cycle):
        for k in range(1, DEPTH + 1):
            rows(level(cycle, k - 1), level(cycle, k), top + k, height - 2 * k)

    def rim(cycle, start, step):
        rows(level(cycle, 0), level(cycle, 1), start + step, DEPTH)

        def two(j, carry):
            at = start + step * (2 * j + 2)
            rows(level(cycle, 1), level(cycle, 2), at, DEPTH)
            rows(level(cycle, 2), level(cycle, 1), at + step, DEPTH)
            return carry
        lax.fori_loop(0, DEPTH // 2 - 1, two, 0)
        rows(level(cycle, 1), level(cycle, 2), start + step * DEPTH, DEPTH)

    def upper_rim(cycle):
        rim(cycle, 0, 1)

    def lower_rim(cycle):
        rim(cycle, bottom, -1)

    pieces = ((DEPTH, height - 2 * DEPTH), (0, DEPTH), (height - DEPTH, DEPTH))

    def mixing(cycle, piece, action):
        start, count = pieces[piece]
        mine = fields.at[3 * cycle + 2, pl.ds(top + start, count)]
        index = 6 + 8 * cycle + 2 * piece
        for side, (exists, shift) in enumerate(((has_lower, -1), (has_upper, 1))):
            @pl.when(exists)
            def _():
                copy = remote(index + side, mine, beside.at[cycle, 1 - side, pl.ds(start, count)], {"ladder": place + shift})
                if action == "start":
                    copy.start()
                elif action == "sent":
                    copy.wait_send()

    def arrive(cycle, piece):
        start, count = pieces[piece]
        index = 6 + 8 * cycle + 2 * piece
        for side, exists in enumerate((has_lower, has_upper)):
            @pl.when(exists)
            def _():
                spot = beside.at[cycle, side, pl.ds(start, count)]
                remote(index + 1 - side, spot, spot, {"ladder": place + (2 * side - 1)}).wait_recv()

    lower_w = mix_ref[0, 0]
    upper_w = mix_ref[0, 1]
    own_w = 1.0 - lower_w - upper_w

    def mixed(cycle, piece, put):
        start, count = pieces[piece]
        for r in range(start, start + count):
            for v in range(halves):
                p = fields[3 * cycle + 2, top + r, v]
                lower = jnp.where(has_lower, beside[cycle, 0, r, v], p)
                upper = jnp.where(has_upper, beside[cycle, 1, r, v], p)
                put(r, v, own_w * p + lower_w * lower + upper_w * upper)

    def next_field(r, v, value):
        fields[3, top + r, v] = value

    def output(r, v, value):
        ostage[pl.ds(v * height + r, SUBS, stride=halves * height), :] = value

    pyramid(0)
    mixing(0, 0, "start")
    coef_up.wait_recv()
    pass_up = remote(4, coef.at[core, pl.ds(bottom, wide)], coef.at[core, pl.ds(bottom, wide)], {"ladder": partner})
    pass_up.start()
    coef_down.wait_recv()
    pass_down = remote(5, coef.at[core, pl.ds(1, wide)], coef.at[core, pl.ds(1, wide)], {"ladder": partner})
    pass_down.start()
    halo_down.wait_recv()
    pass_down.wait_recv()
    upper_rim(0)
    mixing(0, 1, "start")
    halo_up.wait_recv()
    pass_up.wait_recv()
    lower_rim(0)
    mixing(0, 2, "start")
    next_up, next_down = halo(12, fields.at[3])
    arrive(0, 1)
    mixed(0, 1, next_field)
    next_up.start()
    arrive(0, 2)
    mixed(0, 2, next_field)
    next_down.start()
    arrive(0, 0)
    mixed(0, 0, next_field)

    pyramid(1)
    mixing(1, 0, "start")
    next_down.wait_recv()
    upper_rim(1)
    mixing(1, 1, "start")
    next_up.wait_recv()
    lower_rim(1)
    mixing(1, 2, "start")
    for piece in range(3):
        arrive(1, piece)
        mixed(1, piece, output)
    stores = []
    for j in range(blocks):
        copy = pltpu.make_async_copy(
            ostage.at[pl.ds(j * height, height), :],
            out_hbm.at[0, :, pl.ds(j * LANES, LANES)],
            load_sem.at[0, j],
        )
        copy.start()
        stores.append(copy)
    for copy in (coef_up, coef_down, halo_up, halo_down, pass_up, pass_down, next_up, next_down):
        copy.wait_send()
    for cycle in range(CYCLES):
        for piece in range(3):
            mixing(cycle, piece, "sent")
    for copy in stores:
        copy.wait()


def body(initial, mobility, tilt, drift, mix_weights):
    n_ladder = lax.axis_size("ladder")
    n_space = lax.axis_size("space")
    _, height, cols = initial.shape
    blocks = cols // LANES
    halves = blocks // SUBS
    full = height + 2 * DEPTH
    f32 = jnp.float32
    hbm = pl.BlockSpec(memory_space=pl.ANY)
    return pl.pallas_call(
        functools.partial(kernel, (n_ladder, n_space, height, halves, blocks)),
        out_shape=jax.ShapeDtypeStruct(initial.shape, f32),
        in_specs=[hbm, hbm, hbm, pl.BlockSpec(memory_space=pltpu.VMEM), pl.BlockSpec(memory_space=pltpu.SMEM)],
        out_specs=hbm,
        scratch_shapes=[
            pltpu.VMEM((3, blocks * height, LANES), f32),
            pltpu.VMEM((2, full, halves, SUBS, LANES), f32),
            pltpu.VMEM((3 * CYCLES, full, halves, SUBS, LANES), f32),
            pltpu.VMEM((CYCLES, 2, height, halves, SUBS, LANES), f32),
            pltpu.VMEM((blocks * height, LANES), f32),
            pltpu.SemaphoreType.DMA((3, blocks)),
            pltpu.SemaphoreType.DMA((20,)),
            pltpu.SemaphoreType.DMA((20,)),
        ],
        compiler_params=pltpu.CompilerParams(collective_id=0, has_side_effects=True),
    )(initial, mobility, tilt, drift.reshape(blocks, LANES), mix_weights)


def solution(mesh):
    in_specs = (
        P("ladder", "space", None),
        P("space", None),
        P("space", None),
        P(),
        P("ladder", None),
    )
    out_specs = P("ladder", "space", None)
    return jax.shard_map(body, mesh=mesh, in_specs=in_specs, out_specs=out_specs, check_vma=False)
```

```python
import functools

import jax
import jax.numpy as jnp
from jax import lax
from jax.experimental import pallas as pl
from jax.experimental.pallas import tpu as pltpu
from jax.sharding import PartitionSpec as P

CYCLES = 2
DEPTH = 12
LANES = 128
SUBS = 8
STRIP = 4
BLOCK = 4
MESH = pl.DeviceIdType.MESH


def kernel(sizes, init_hbm, mob_hbm, tilt_hbm, drift_ref, mix_ref, out_hbm,
           stage, coef, fields, beside, ostage, load_sem, send_sem, recv_sem):
    n_ladder, n_space, height, halves, blocks = sizes
    place = lax.axis_index("ladder")
    slab = lax.axis_index("space")
    prev = lax.rem(slab + n_space - 1, n_space)
    following = lax.rem(slab + 1, n_space)
    strips = DEPTH // STRIP
    group = 4 if n_ladder % 4 == 0 else 2
    member = lax.rem(place, group)
    has_lower = place > 0
    has_upper = place < n_ladder - 1
    top, bottom = DEPTH, DEPTH + height

    sources = (mob_hbm, tilt_hbm, init_hbm.at[0])
    loads = []
    for a, src in enumerate(sources):
        for j in range(blocks):
            copy = pltpu.make_async_copy(
                src.at[:, pl.ds(j * LANES, LANES)],
                stage.at[a, pl.ds(j * height, height), :],
                load_sem.at[a, j],
            )
            copy.start()
            loads.append(copy)

    barrier = pltpu.get_barrier_semaphore()
    for target in (prev, following):
        pl.semaphore_signal(barrier, inc=1, device_id={"space": target}, device_id_type=MESH)

    around_me = [lax.rem(place + n_ladder - 1, n_ladder), lax.rem(place + 1, n_ladder)]
    around_me += [place - member + lax.rem(member + hop, group) for hop in range(1, group)]
    for target in around_me:
        pl.semaphore_signal(barrier, inc=1, device_id={"ladder": target}, device_id_type=MESH)

    def remote(index, src, dst, device):
        return pltpu.make_async_remote_copy(
            src_ref=src, dst_ref=dst, send_sem=send_sem.at[index], recv_sem=recv_sem.at[index],
            device_id=device, device_id_type=MESH)

    def spread(a, dst, scale):
        for r in range(height):
            for v in range(halves):
                tile = stage[a, pl.ds(v * height + r, SUBS, stride=halves * height), :]
                dst[top + r, v] = tile * scale if scale is not None else tile

    for copy in loads[: 2 * blocks]:
        copy.wait()
    spread(0, coef.at[0], 0.1)
    spread(1, coef.at[1], None)

    pl.semaphore_wait(barrier, 2 + len(around_me))

    kind = lax.rem(member, 2)
    share = 2 * DEPTH // group
    offset = lax.div(member, 2) * share
    near_top = coef.at[kind, pl.ds(top + offset, share)]
    near_bottom = coef.at[kind, pl.ds(bottom - DEPTH + offset, share)]
    far_top = coef.at[kind, pl.ds(offset, share)]
    far_bottom = coef.at[kind, pl.ds(bottom + offset, share)]
    coef_up = remote(0, near_top, far_bottom, {"space": prev})
    coef_down = remote(1, near_bottom, far_top, {"space": following})
    coef_up.start()
    coef_down.start()
    for copy in loads[2 * blocks:]:
        copy.wait()
    spread(2, fields.at[0], None)

    def halo(cycle, t):
        f = fields.at[3 * cycle]
        near = t * STRIP
        far = DEPTH - STRIP - t * STRIP
        index = 2 + 6 * cycle + 2 * t
        up = remote(index, f.at[pl.ds(top + near, STRIP)], f.at[pl.ds(bottom + near, STRIP)], {"space": prev})
        down = remote(index + 1, f.at[pl.ds(bottom - STRIP - near, STRIP)], f.at[pl.ds(far, STRIP)], {"space": following})
        return up, down

    halos = [[halo(cycle, t) for t in range(strips)] for cycle in range(CYCLES)]
    for t in range(strips):
        for copy in halos[0][t]:
            copy.start()

    passes = []
    for hop in range(1, group):
        other = {"ladder": place - member + lax.rem(member + hop, group)}
        index = 14 + 2 * (hop - 1)
        passes.append((remote(index, far_bottom, far_bottom, other), remote(index + 1, far_top, far_top, other)))

    lane = lax.broadcasted_iota(jnp.int32, (SUBS, LANES), 1)
    at_first = lane == 0
    at_last = lane == LANES - 1
    drifts = [drift_ref[pl.ds(v, SUBS, stride=halves), :] for v in range(halves)]
    speeds = [jnp.abs(u) for u in drifts]
    rises = [u > 0.0 for u in drifts]

    def rows(src, dst, base, many=STRIP):
        tiles = [[src[base - 1 + r, v] for v in range(halves)] for r in range(many + 2)]
        for r in range(many):
            below, here, above = tiles[r], tiles[r + 1], tiles[r + 2]
            right = [pltpu.roll(here[v], 1, 1) for v in range(halves)]
            left = [pltpu.roll(here[v], LANES - 1, 1) for v in range(halves)]
            before = [pltpu.roll(right[-1], 1, 0)] + right[:-1]
            after = left[1:] + [pltpu.roll(left[0], SUBS - 1, 0)]
            for v in range(halves):
                p = here[v]
                side = jnp.where(at_first, before[v], right[v]) + jnp.where(at_last, after[v], left[v])
                around = side + (below[v] + above[v]) + coef[1, base + r, v]
                drive = around - p * (p * p + 3.0)
                carried = jnp.where(rises[v], below[v], above[v]) - p
                dst[base + r, v] = p + speeds[v] * carried + coef[0, base + r, v] * drive

    def level(cycle, k):
        return fields.at[3 * cycle + (0 if k == 0 else 1 + (k + 1) % 2)]

    def pyramid(cycle):
        for k in range(1, DEPTH + 1):
            src, dst = level(cycle, k - 1), level(cycle, k)
            count = height - 2 * k
            start = top + k

            def some(c, carry):
                rows(src, dst, start + c * BLOCK, BLOCK)
                return carry
            lax.fori_loop(0, count // BLOCK, some, 0)
            if count % BLOCK:
                rows(src, dst, start + count - count % BLOCK, count % BLOCK)

    def strip(cycle, t):
        low = DEPTH - STRIP - t * STRIP
        high = bottom + t * STRIP

        def both(src, dst, k):
            rows(src, dst, low + k)
            rows(src, dst, high - k)

        both(level(cycle, 0), level(cycle, 1), 1)

        def two(j, carry):
            both(level(cycle, 1), level(cycle, 2), 2 * j + 2)
            both(level(cycle, 2), level(cycle, 1), 2 * j + 3)
            return carry
        lax.fori_loop(0, DEPTH // 2 - 1, two, 0)
        both(level(cycle, 1), level(cycle, 2), DEPTH)

    inner = DEPTH - STRIP
    pieces = [[(inner, height - 2 * inner)]]
    for t in range(1, strips):
        pieces.append([(inner - t * STRIP, STRIP), (height - inner + (t - 1) * STRIP, STRIP)])
    numbers = {}
    for cycle in range(CYCLES):
        for piece in [p for group_of in pieces for p in group_of]:
            numbers[cycle, piece] = 14 + 2 * (group - 1) + 2 * len(numbers)

    def mixing(cycle, piece, action):
        start, count = piece
        mine = fields.at[3 * cycle + 2, pl.ds(top + start, count)]
        index = numbers[cycle, piece]
        for side, (exists, shift) in enumerate(((has_lower, -1), (has_upper, 1))):
            @pl.when(exists)
            def _():
                copy = remote(index + side, mine, beside.at[cycle, 1 - side, pl.ds(start, count)], {"ladder": place + shift})
                if action == "start":
                    copy.start()
                elif action == "sent":
                    copy.wait_send()

    def arrive(cycle, piece):
        start, count = piece
        index = numbers[cycle, piece]
        for side, exists in enumerate((has_lower, has_upper)):
            @pl.when(exists)
            def _():
                spot = beside.at[cycle, side, pl.ds(start, count)]
                remote(index + 1 - side, spot, spot, {"ladder": place + (2 * side - 1)}).wait_recv()

    lower_w = mix_ref[0, 0]
    upper_w = mix_ref[0, 1]
    own_w = 1.0 - lower_w - upper_w

    def mixed(cycle, piece, put):
        start, count = piece
        for r in range(start, start + count):
            for v in range(halves):
                p = fields[3 * cycle + 2, top + r, v]
                lower = jnp.where(has_lower, beside[cycle, 0, r, v], p)
                upper = jnp.where(has_upper, beside[cycle, 1, r, v], p)
                put(r, v, own_w * p + lower_w * lower + upper_w * upper)

    def next_field(r, v, value):
        fields[3, top + r, v] = value

    def output(r, v, value):
        ostage[pl.ds(v * height + r, SUBS, stride=halves * height), :] = value

    def strips_of(cycle):
        for t in range(strips):
            for copy in halos[cycle][t]:
                copy.wait_recv()
            if cycle == 0 and t == 0:
                for up, down in passes:
                    up.wait_recv()
                    down.wait_recv()
            strip(cycle, t)
            for piece in pieces[t]:
                mixing(cycle, piece, "start")

    pyramid(0)
    coef_up.wait_recv()
    for up, down in passes:
        up.start()
    coef_down.wait_recv()
    for up, down in passes:
        down.start()
    strips_of(0)
    for t in range(strips):
        for piece in pieces[t]:
            arrive(0, piece)
            mixed(0, piece, next_field)
        for copy in halos[1][strips - 1 - t]:
            copy.start()

    pyramid(1)
    strips_of(1)
    for t in range(strips):
        for piece in pieces[t]:
            arrive(1, piece)
            mixed(1, piece, output)
    stores = []
    for j in range(blocks):
        copy = pltpu.make_async_copy(
            ostage.at[pl.ds(j * height, height), :],
            out_hbm.at[0, :, pl.ds(j * LANES, LANES)],
            load_sem.at[0, j],
        )
        copy.start()
        stores.append(copy)
    for copy in (coef_up, coef_down):
        copy.wait_send()
    for pairs in halos + [passes]:
        for pair in pairs:
            for copy in pair:
                copy.wait_send()
    for cycle, piece in numbers:
        mixing(cycle, piece, "sent")
    for copy in stores:
        copy.wait()


def body(initial, mobility, tilt, drift, mix_weights):
    n_ladder = lax.axis_size("ladder")
    n_space = lax.axis_size("space")
    _, height, cols = initial.shape
    blocks = cols // LANES
    halves = blocks // SUBS
    full = height + 2 * DEPTH
    f32 = jnp.float32
    hbm = pl.BlockSpec(memory_space=pl.ANY)
    return pl.pallas_call(
        functools.partial(kernel, (n_ladder, n_space, height, halves, blocks)),
        out_shape=jax.ShapeDtypeStruct(initial.shape, f32),
        in_specs=[hbm, hbm, hbm, pl.BlockSpec(memory_space=pltpu.VMEM), pl.BlockSpec(memory_space=pltpu.SMEM)],
        out_specs=hbm,
        scratch_shapes=[
            pltpu.VMEM((3, blocks * height, LANES), f32),
            pltpu.VMEM((2, full, halves, SUBS, LANES), f32),
            pltpu.VMEM((3 * CYCLES, full, halves, SUBS, LANES), f32),
            pltpu.VMEM((CYCLES, 2, height, halves, SUBS, LANES), f32),
            pltpu.VMEM((blocks * height, LANES), f32),
            pltpu.SemaphoreType.DMA((3, blocks)),
            pltpu.SemaphoreType.DMA((48,)),
            pltpu.SemaphoreType.DMA((48,)),
        ],
        compiler_params=pltpu.CompilerParams(collective_id=0, has_side_effects=True),
    )(initial, mobility, tilt, drift.reshape(blocks, LANES), mix_weights)


def solution(mesh):
    in_specs = (
        P("ladder", "space", None),
        P("space", None),
        P("space", None),
        P(),
        P("ladder", None),
    )
    out_specs = P("ladder", "space", None)
    return jax.shard_map(body, mesh=mesh, in_specs=in_specs, out_specs=out_specs, check_vma=False)
```

```python
import functools

import jax
import jax.numpy as jnp
from jax import lax
from jax.experimental import pallas as pl
from jax.experimental.pallas import tpu as pltpu
from jax.sharding import PartitionSpec as P

CYCLES = 2
DEPTH = 12
LANES = 128
SUBS = 8
CHUNK = 4
MESH = pl.DeviceIdType.MESH


def kernel(sizes, init_hbm, mob_hbm, tilt_hbm, drift_ref, mix_ref, out_hbm,
           stage, coef, fields, beside, ostage, load_sem, send_sem, recv_sem):
    n_ladder, n_space, height, halves, blocks = sizes
    place = lax.axis_index("ladder")
    slab = lax.axis_index("space")
    prev = lax.rem(slab + n_space - 1, n_space)
    following = lax.rem(slab + 1, n_space)
    core = lax.rem(place, 2)
    partner = place + 1 - 2 * core
    has_lower = place > 0
    has_upper = place < n_ladder - 1
    top, bottom = DEPTH, DEPTH + height

    sources = (mob_hbm, tilt_hbm, init_hbm.at[0])
    loads = []
    for a, src in enumerate(sources):
        for j in range(blocks):
            copy = pltpu.make_async_copy(
                src.at[:, pl.ds(j * LANES, LANES)],
                stage.at[a, pl.ds(j * height, height), :],
                load_sem.at[a, j],
            )
            copy.start()
            loads.append(copy)

    barrier = pltpu.get_barrier_semaphore()
    for target in (prev, following):
        pl.semaphore_signal(barrier, inc=1, device_id={"space": target}, device_id_type=MESH)

    for target in (lax.rem(place + n_ladder - 1, n_ladder), lax.rem(place + 1, n_ladder)):
        pl.semaphore_signal(barrier, inc=1, device_id={"ladder": target}, device_id_type=MESH)

    def remote(index, src, dst, device):
        return pltpu.make_async_remote_copy(
            src_ref=src, dst_ref=dst, send_sem=send_sem.at[index], recv_sem=recv_sem.at[index],
            device_id=device, device_id_type=MESH)

    def spread(a, dst, scale):
        for r in range(height):
            for v in range(halves):
                tile = stage[a, pl.ds(v * height + r, SUBS, stride=halves * height), :]
                dst[top + r, v] = tile * scale if scale is not None else tile

    wide = DEPTH - 1
    for copy in loads[: 2 * blocks]:
        copy.wait()
    spread(0, coef.at[0], 0.1)
    spread(1, coef.at[1], None)

    pl.semaphore_wait(barrier, 4)

    coef_up = remote(0, coef.at[core, pl.ds(top, wide)], coef.at[core, pl.ds(bottom, wide)], {"space": prev})
    coef_down = remote(1, coef.at[core, pl.ds(bottom - wide, wide)], coef.at[core, pl.ds(1, wide)], {"space": following})
    coef_up.start()
    coef_down.start()
    for copy in loads[2 * blocks:]:
        copy.wait()
    spread(2, fields.at[0], None)

    def halo(index, f):
        up = remote(index, f.at[pl.ds(top, DEPTH)], f.at[pl.ds(bottom, DEPTH)], {"space": prev})
        down = remote(index + 1, f.at[pl.ds(bottom - DEPTH, DEPTH)], f.at[pl.ds(0, DEPTH)], {"space": following})
        return up, down

    halo_up, halo_down = halo(2, fields.at[0])
    halo_up.start()
    halo_down.start()

    lane = lax.broadcasted_iota(jnp.int32, (SUBS, LANES), 1)
    at_first = lane == 0
    at_last = lane == LANES - 1
    drifts = [drift_ref[pl.ds(v, SUBS, stride=halves), :] for v in range(halves)]
    speeds = [jnp.abs(u) for u in drifts]
    rises = [u > 0.0 for u in drifts]

    def rows(src, dst, lo, count):
        for first in range(0, count, CHUNK):
            many = min(CHUNK, count - first)
            base = lo + first
            tiles = [[src[base - 1 + r, v] for v in range(halves)] for r in range(many + 2)]
            for r in range(many):
                below, here, above = tiles[r], tiles[r + 1], tiles[r + 2]
                right = [pltpu.roll(here[v], 1, 1) for v in range(halves)]
                left = [pltpu.roll(here[v], LANES - 1, 1) for v in range(halves)]
                before = [pltpu.roll(right[-1], 1, 0)] + right[:-1]
                after = left[1:] + [pltpu.roll(left[0], SUBS - 1, 0)]
                for v in range(halves):
                    p = here[v]
                    side = jnp.where(at_first, before[v], right[v]) + jnp.where(at_last, after[v], left[v])
                    around = side + (below[v] + above[v]) + coef[1, base + r, v]
                    drive = around - p * (p * p + 3.0)
                    carried = jnp.where(rises[v], below[v], above[v]) - p
                    dst[base + r, v] = p + speeds[v] * carried + coef[0, base + r, v] * drive

    def level(cycle, k):
        return fields.at[3 * cycle + (0 if k == 0 else 1 + (k + 1) % 2)]

    def pyramid(cycle):
        for k in range(1, DEPTH + 1):
            rows(level(cycle, k - 1), level(cycle, k), top + k, height - 2 * k)

    def rims(cycle):
        for k in range(1, DEPTH + 1):
            rows(level(cycle, k - 1), level(cycle, k), k, DEPTH)
            rows(level(cycle, k - 1), level(cycle, k), bottom - k, DEPTH)

    pieces = ((DEPTH, height - 2 * DEPTH), (0, DEPTH), (height - DEPTH, DEPTH))

    def mixing(cycle, piece, action):
        start, count = pieces[piece]
        mine = fields.at[3 * cycle + 2, pl.ds(top + start, count)]
        index = 6 + 8 * cycle + 2 * piece
        for side, (exists, shift) in enumerate(((has_lower, -1), (has_upper, 1))):
            @pl.when(exists)
            def _():
                copy = remote(index + side, mine, beside.at[cycle, 1 - side, pl.ds(start, count)], {"ladder": place + shift})
                if action == "start":
                    copy.start()
                elif action == "sent":
                    copy.wait_send()

    def arrive(cycle, piece):
        start, count = pieces[piece]
        index = 6 + 8 * cycle + 2 * piece
        for side, exists in enumerate((has_lower, has_upper)):
            @pl.when(exists)
            def _():
                spot = beside.at[cycle, side, pl.ds(start, count)]
                remote(index + 1 - side, spot, spot, {"ladder": place + (2 * side - 1)}).wait_recv()

    lower_w = mix_ref[0, 0]
    upper_w = mix_ref[0, 1]
    own_w = 1.0 - lower_w - upper_w

    def mixed(cycle, piece, put):
        start, count = pieces[piece]
        for r in range(start, start + count):
            for v in range(halves):
                p = fields[3 * cycle + 2, top + r, v]
                lower = jnp.where(has_lower, beside[cycle, 0, r, v], p)
                upper = jnp.where(has_upper, beside[cycle, 1, r, v], p)
                put(r, v, own_w * p + lower_w * lower + upper_w * upper)

    def next_field(r, v, value):
        fields[3, top + r, v] = value

    def output(r, v, value):
        ostage[pl.ds(v * height + r, SUBS, stride=halves * height), :] = value

    pyramid(0)
    mixing(0, 0, "start")
    coef_up.wait_recv()
    pass_up = remote(4, coef.at[core, pl.ds(bottom, wide)], coef.at[core, pl.ds(bottom, wide)], {"ladder": partner})
    pass_up.start()
    coef_down.wait_recv()
    pass_down = remote(5, coef.at[core, pl.ds(1, wide)], coef.at[core, pl.ds(1, wide)], {"ladder": partner})
    pass_down.start()
    halo_down.wait_recv()
    pass_down.wait_recv()
    halo_up.wait_recv()
    pass_up.wait_recv()
    rims(0)
    mixing(0, 1, "start")
    mixing(0, 2, "start")
    next_up, next_down = halo(12, fields.at[3])
    arrive(0, 1)
    mixed(0, 1, next_field)
    next_up.start()
    arrive(0, 2)
    mixed(0, 2, next_field)
    next_down.start()
    arrive(0, 0)
    mixed(0, 0, next_field)

    pyramid(1)
    mixing(1, 0, "start")
    next_down.wait_recv()
    next_up.wait_recv()
    rims(1)
    mixing(1, 1, "start")
    mixing(1, 2, "start")
    for piece in range(3):
        arrive(1, piece)
        mixed(1, piece, output)
    stores = []
    for j in range(blocks):
        copy = pltpu.make_async_copy(
            ostage.at[pl.ds(j * height, height), :],
            out_hbm.at[0, :, pl.ds(j * LANES, LANES)],
            load_sem.at[0, j],
        )
        copy.start()
        stores.append(copy)
    for copy in (coef_up, coef_down, halo_up, halo_down, pass_up, pass_down, next_up, next_down):
        copy.wait_send()
    for cycle in range(CYCLES):
        for piece in range(3):
            mixing(cycle, piece, "sent")
    for copy in stores:
        copy.wait()


def body(initial, mobility, tilt, drift, mix_weights):
    n_ladder = lax.axis_size("ladder")
    n_space = lax.axis_size("space")
    _, height, cols = initial.shape
    blocks = cols // LANES
    halves = blocks // SUBS
    full = height + 2 * DEPTH
    f32 = jnp.float32
    hbm = pl.BlockSpec(memory_space=pl.ANY)
    return pl.pallas_call(
        functools.partial(kernel, (n_ladder, n_space, height, halves, blocks)),
        out_shape=jax.ShapeDtypeStruct(initial.shape, f32),
        in_specs=[hbm, hbm, hbm, pl.BlockSpec(memory_space=pltpu.VMEM), pl.BlockSpec(memory_space=pltpu.SMEM)],
        out_specs=hbm,
        scratch_shapes=[
            pltpu.VMEM((3, blocks * height, LANES), f32),
            pltpu.VMEM((2, full, halves, SUBS, LANES), f32),
            pltpu.VMEM((3 * CYCLES, full, halves, SUBS, LANES), f32),
            pltpu.VMEM((CYCLES, 2, height, halves, SUBS, LANES), f32),
            pltpu.VMEM((blocks * height, LANES), f32),
            pltpu.SemaphoreType.DMA((3, blocks)),
            pltpu.SemaphoreType.DMA((20,)),
            pltpu.SemaphoreType.DMA((20,)),
        ],
        compiler_params=pltpu.CompilerParams(collective_id=0, has_side_effects=True),
    )(initial, mobility, tilt, drift.reshape(blocks, LANES), mix_weights)


def solution(mesh):
    in_specs = (
        P("ladder", "space", None),
        P("space", None),
        P("space", None),
        P(),
        P("ladder", None),
    )
    out_specs = P("ladder", "space", None)
    return jax.shard_map(body, mesh=mesh, in_specs=in_specs, out_specs=out_specs, check_vma=False)
```
